32 devices in a mesh: groups: 1, replica: 32 (over z, y, x, core).
Axes of the slice: x: 2, y: 2, z: 4, core: 2. Of those that a mesh axis runs over, the one named last changes fastest.
Arguments:
- queries: bfloat16 [8192, 1024], P(('groups', 'replica')), may hold values from -15 to 15
- suffix_kv: bfloat16 [8192, 256], P(('groups', 'replica')), may hold values from -6 to 6
- own_cache: bfloat16 [16384, 256], P(('groups', 'replica')), may hold values from -6 to 6
- ctx_len: int32 [32], P(('groups', 'replica')), may hold values from 64 to 512, as said below
- prefix_cache: bfloat16 [131072, 256], P(('groups', 'replica')), may hold values from -18 to 18
- owners: int32 [2], P('groups'), may hold values from 0 to 31, as said below
- readers: int32 [32], P('groups'), may hold values from 0 to 1
- kv_pool: bfloat16 [1024, 128, 256], P(('groups', 'replica')), may hold values from -6 to 6
- mig_target: int32 [32, 32], P(('groups', 'replica')), may hold values from 0 to 31, as said below
- mig_block: int32 [32, 32], P(('groups', 'replica')), may hold values from 0 to 31, each once within a row
- mig_count: int32 [32], P(('groups', 'replica')), may hold values from 8 to 32, as said below
Outputs:
- attended: bfloat16 [8192, 1024], P(('groups', 'replica'))
The draws below stay inside these ranges and needn't reach their ends.
Inputs may be any that keep to these rules, and one draw needn't show every extreme that they name: `owners`: 2 different replicas; replica 32 - 1 owns one prefix in every draw. `ctx_len`: the largest value is 512 in every draw. `mig_target`: each row names every replica once, so one source sends at most one block to one target; in every draw one replica is the first entry of every row. `mig_block`: each row names every block of the source's pool once. `mig_count`: the largest value is 32 in every draw.
All inputs are finite; a program needn't handle non-finite values.
Results may differ from the reference program's by a relative error of at most 0.0019.
Values may be sent and summed in bfloat16 or wider, within the bound.
A program may use at most 128 MiB of HBM per device.

```python
import math
import jax
import jax.numpy as jnp
import numpy as np
from jax import lax

HD = 128
HQ = 8
SUF = 256
PL = 4096
CTX = 512
BLK = 128
NP = 2
NB = 32
N_REPLICA = 32


def sign_pattern(key):
    flips = jax.random.bernoulli(jax.random.fold_in(key, 991), 0.5, (HD,))
    return jnp.where(flips, 1.0, -1.0).astype(jnp.float32)


def crossing_pattern(key):
    balanced = jnp.where(jnp.arange(HD) < HD // 2, 1.0, -1.0).astype(jnp.float32)
    mixed = jax.random.permutation(jax.random.fold_in(key, 993), balanced)
    return (sign_pattern(key) * mixed).astype(jnp.float32)


def column_scale():
    return jnp.where(jnp.arange(2 * HD) < HD, 0.6, 1.0).astype(jnp.float32)


def cache_rows(key, salt, shape):
    drawn = jnp.clip(jax.random.normal(jax.random.fold_in(key, salt), shape, jnp.float32), -6.0, 6.0)
    return (drawn * column_scale()).astype(jnp.bfloat16)


def draw_suffix_kv(key, part):
    return cache_rows(key, 41, (N_REPLICA * SUF, 2 * HD))


def draw_own_cache(key, part):
    return cache_rows(key, 43, (N_REPLICA * CTX, 2 * HD))


def draw_kv_pool(key, part):
    return cache_rows(key, 47, (N_REPLICA * NB, BLK, 2 * HD))


def draw_queries(key, part):
    drawn = jnp.clip(4.0 * jax.random.normal(jax.random.fold_in(key, 11), (N_REPLICA, SUF, HQ, HD), jnp.float32), -15.0, 15.0)
    return drawn.reshape(N_REPLICA * SUF, HQ * HD).astype(jnp.bfloat16)


def draw_prefix_cache(key, part):
    drawn = jnp.clip(jax.random.normal(jax.random.fold_in(key, 23), (N_REPLICA, PL, 2 * HD), jnp.float32), -6.0, 6.0)
    drawn = drawn * column_scale()[None, None, :]
    planted = jax.random.randint(jax.random.fold_in(key, 53), (N_REPLICA,), 2, PL).astype(jnp.int32)
    rows = jnp.arange(PL, dtype=jnp.int32)
    columns = jnp.arange(2 * HD, dtype=jnp.int32)
    large_key = jnp.concatenate([18.0 * crossing_pattern(key), jnp.zeros((HD,), jnp.float32)])
    select = (rows[None, :, None] == planted[:, None, None]) & (columns[None, None, :] < HD)
    drawn = jnp.where(select, large_key[None, None, :], drawn)
    return drawn.reshape(N_REPLICA * PL, 2 * HD).astype(jnp.bfloat16)


def draw_owners(key, part):
    others = jax.random.permutation(jax.random.fold_in(key, 31), N_REPLICA - 1)[:NP - 1].astype(jnp.int32)
    listed = jnp.concatenate([others, jnp.full((1,), N_REPLICA - 1, jnp.int32)])
    order = jax.random.permutation(jax.random.fold_in(key, 37), NP)
    return listed[order].astype(jnp.int32)


def draw_ctx_len(key, part):
    lengths = jax.random.randint(jax.random.fold_in(key, 3), (N_REPLICA,), CTX // 8, CTX + 1).astype(jnp.int32)
    picked = jax.random.randint(jax.random.fold_in(key, 4), (), 0, N_REPLICA)
    return lengths.at[picked].set(CTX).astype(jnp.int32)


def draw_mig_target(key, part):
    first = jax.random.randint(jax.random.fold_in(key, 5), (), 0, N_REPLICA)
    columns = jnp.arange(N_REPLICA, dtype=jnp.int32)
    ranking = jax.random.randint(jax.random.fold_in(key, 6), (N_REPLICA, N_REPLICA), 0, 2 ** 20) * N_REPLICA + columns[None, :]
    ranking = jnp.where(columns[None, :] == first, -1, ranking)
    return jnp.argsort(ranking, axis=1, stable=True).astype(jnp.int32)


def draw_mig_count(key, part):
    counts = jax.random.randint(jax.random.fold_in(key, 7), (N_REPLICA,), N_REPLICA // 4, N_REPLICA + 1).astype(jnp.int32)
    picked = jax.random.randint(jax.random.fold_in(key, 8), (), 0, N_REPLICA)
    return counts.at[picked].set(N_REPLICA).astype(jnp.int32)


def plant(values, rng, least, top_value):
    extent = values.shape
    place = [jax.random.randint(jax.random.fold_in(rng, axis), (), 0, extent[axis]) for axis in range(len(extent))]
    values = values.at[tuple(place)].set(least)
    longest = extent.index(max(extent))
    place[longest] = (place[longest] + 1) % extent[longest]
    return values.at[tuple(place)].set(top_value)


def rank_bounds(count, lean):
    weights = [(1 << 20) // math.isqrt(rank ** lean) + 1 for rank in range(1, count + 1)]
    width = 1 + sum(weights) // (1 << 30)
    return np.cumsum(np.array([max(1, weight // width) for weight in weights]))


def ranked(key, extent, count, slope):
    listing = rank_bounds(count, slope)
    lot = jax.random.randint(jax.random.fold_in(key, 1), extent, 0, int(listing[count - 1]))
    standing = jnp.searchsorted(jnp.asarray(listing, jnp.int32), lot, side="right")
    return jax.random.permutation(jax.random.fold_in(key, 2), count)[standing].astype(jnp.int32)


def setup_inputs(seed: int = 0, part: int = 0) -> dict:
    key_list = jax.random.split(jax.random.key(seed), 12)
    part_splits = jax.random.split(jax.random.fold_in(key_list[11], part), 12)
    queries = draw_queries(jax.random.fold_in(jax.random.fold_in(key_list[11], part), 71), part)
    suffix_kv = draw_suffix_kv(jax.random.fold_in(jax.random.fold_in(key_list[11], part), 71), part)
    own_cache = draw_own_cache(jax.random.fold_in(jax.random.fold_in(key_list[11], part), 71), part)
    ctx_len = draw_ctx_len(jax.random.fold_in(jax.random.fold_in(key_list[11], part), 71), part)
    prefix_cache = draw_prefix_cache(jax.random.fold_in(jax.random.fold_in(key_list[11], part), 71), part)
    owners = draw_owners(jax.random.fold_in(jax.random.fold_in(key_list[11], part), 71), part)
    readers = plant(ranked(part_splits[6], (N_REPLICA,), NP, 2), jax.random.fold_in(part_splits[6], 3), 0, NP - 1).astype(jnp.int32)
    kv_pool = draw_kv_pool(jax.random.fold_in(jax.random.fold_in(key_list[11], part), 71), part)
    mig_target = draw_mig_target(jax.random.fold_in(jax.random.fold_in(key_list[11], part), 71), part)
    mig_block = jax.vmap(lambda own: jax.random.permutation(own, NB))(jax.random.split(part_splits[9], N_REPLICA)).reshape((N_REPLICA, NB)).astype(jnp.int32)
    mig_count = draw_mig_count(jax.random.fold_in(jax.random.fold_in(key_list[11], part), 71), part)
    return {"queries": queries, "suffix_kv": suffix_kv, "own_cache": own_cache, "ctx_len": ctx_len, "prefix_cache": prefix_cache, "owners": owners, "readers": readers, "kv_pool": kv_pool, "mig_target": mig_target, "mig_block": mig_block, "mig_count": mig_count}


def reference(queries, suffix_kv, own_cache, ctx_len, prefix_cache, owners, readers, kv_pool, mig_target, mig_block, mig_count):
    prefixes = prefix_cache.reshape(N_REPLICA, PL, 2 * HD)
    pools = kv_pool.reshape(N_REPLICA, NB, BLK, 2 * HD)
    owned = own_cache.reshape(N_REPLICA, CTX, 2 * HD)
    suffixes = suffix_kv.reshape(N_REPLICA, SUF, 2 * HD)
    query_sets = queries.reshape(N_REPLICA, SUF * HQ, HD)
    entries = jnp.arange(N_REPLICA, dtype=jnp.int32)
    source_ids = jnp.arange(N_REPLICA, dtype=jnp.int32)
    entry_live = entries[None, :] < mig_count[:, None]
    row_count = SUF * HQ
    positions = jnp.arange(row_count, dtype=jnp.int32) // HQ
    score_scale = HD ** -0.5

    def attend_replica(replica):
        prefix_rows = prefixes[owners[readers[replica]]]
        matching = (mig_target == replica) & entry_live
        entry_pos = jnp.sum(jnp.where(matching, entries[None, :], 0), axis=1).astype(jnp.int32)
        received = jnp.any(matching, axis=1)
        block_ids = jnp.take_along_axis(mig_block, entry_pos[:, None], axis=1)[:, 0]
        moved = pools[source_ids, block_ids].reshape(N_REPLICA * BLK, 2 * HD)
        moved_mask = jnp.repeat(received, BLK)
        own_rows = owned[replica]
        own_mask = jnp.arange(CTX, dtype=jnp.int32) < ctx_len[replica]
        suffix_rows = suffixes[replica]
        key_values = jnp.concatenate([prefix_rows, moved, own_rows, suffix_rows], axis=0)
        column_mask = jnp.concatenate([jnp.ones((PL,), bool), moved_mask, own_mask, jnp.ones((SUF,), bool)])
        causal = jnp.arange(SUF, dtype=jnp.int32)[None, :] <= positions[:, None]
        allowed = jnp.concatenate([jnp.ones((row_count, PL + N_REPLICA * BLK + CTX), bool), causal], axis=1)
        allowed = allowed & column_mask[None, :]
        scores = lax.dot_general(query_sets[replica], key_values[:, :HD], (((1,), (1,)), ((), ())), preferred_element_type=jnp.float32) * score_scale
        scores = jnp.where(allowed, scores, -jnp.inf)
        row_max = jnp.max(scores, axis=1, keepdims=True)
        exponent = jnp.exp(scores - row_max)
        denominator = jnp.sum(exponent, axis=1, keepdims=True)
        numerator = jnp.dot(exponent.astype(jnp.bfloat16), key_values[:, HD:], preferred_element_type=jnp.float32)
        return (numerator / denominator).astype(jnp.bfloat16).reshape(SUF, HQ * HD)

    attended = lax.map(attend_replica, jnp.arange(N_REPLICA, dtype=jnp.int32))
    return attended.reshape(N_REPLICA * SUF, HQ * HD)
```

```python
import functools
import math

import jax
import jax.numpy as jnp
from jax import lax
from jax.experimental import pallas as pl
from jax.experimental.pallas import tpu as pltpu
from jax.sharding import PartitionSpec as P

DEAD = 64.0
LIMIT = 32.0
MESH = pl.DeviceIdType.MESH


def move_order(replicas):
    top = replicas // 2
    near = 8 if replicas >= 16 else 2

    def key(k):
        return (k % near < 2, k)

    across = sorted(range(top, replicas), key=key)
    within = sorted(range(1, top), key=key)
    order = []
    while across or within:
        if across:
            order.append(across.pop(0))
        if within:
            order.append(within.pop(0))
    return order


def attention_kernel(
    cfg,
    ctx_ref,
    owners_ref,
    readers_ref,
    count_ref,
    target_ref,
    block_ref,
    q_ref,
    suffix_ref,
    own_ref,
    prefix_ref,
    pool_ref,
    o_ref,
    gathered,
    work,
    first_recv,
    later_recv,
    arrived,
    out_blocks,
    codes_vmem,
    codes,
    m_ref,
    l_ref,
    acc_ref,
    rs_send,
    rs_recv,
    ag_send,
    ag_recv,
    st_send,
    st_recv,
    mv_send,
    mv_recv,
    core_send,
    core_recv,
    code_sem,
):
    replicas, prefixes, heads, hd = cfg
    steps = replicas.bit_length() - 1
    prefix_len = prefix_ref.shape[0]
    parts = 2
    part_rows = prefix_len // parts
    piece = part_rows // replicas
    dynamic = prefixes - 1
    orders = [list(range(steps)), list(range(steps))]
    if steps > 2:
        orders[1][1], orders[1][2] = orders[1][2], orders[1][1]
    me = lax.axis_index("replica")
    coef = hd ** (-0.5) * math.log2(math.e)
    order = move_order(replicas)

    def bit_of(device, b):
        return lax.rem(device // (1 << b), 2)

    my_bits = [bit_of(me, b) for b in range(steps)]

    def flip(k):
        device = me
        for b in range(steps):
            if (k >> b) & 1:
                device = device + (1 - 2 * my_bits[b]) * (1 << b)
        return device

    def range_low(device, part, level):
        low = part * part_rows
        for t in range(level):
            low = low + bit_of(device, orders[part][t]) * (part_rows >> (t + 1))
        return low

    def rows_at(low, count):
        return pl.ds(pl.multiple_of(low, piece), count)

    barrier = pltpu.get_barrier_semaphore()

    def greet(i, c):
        pl.semaphore_signal(
            barrier, inc=1, device_id={"replica": lax.rem(me + i, replicas)}, device_id_type=MESH
        )
        return c

    lax.fori_loop(1, replicas, greet, 0)

    n_entries = target_ref.shape[1]
    shape = (replicas, n_entries)
    live = lax.broadcasted_iota(jnp.int32, shape, 1) < count_ref[0]
    hit = (target_ref[...] == lax.broadcasted_iota(jnp.int32, shape, 0)) & live
    found = jnp.sum(jnp.where(hit, block_ref[...] + 1, 0), axis=1, keepdims=True) - 1
    codes_vmem[...] = jnp.broadcast_to(found, codes_vmem.shape)
    code_copy = pltpu.make_async_copy(codes_vmem, codes, code_sem)
    code_copy.start()

    last_at = jnp.int32(0)
    for p in range(prefixes):
        last_at = jnp.where(owners_ref[p] == replicas - 1, p, last_at)
    dynamic_owner = []
    for d in range(dynamic):
        dynamic_owner.append(jnp.where(last_at <= d, owners_ref[d + 1], owners_ref[d]))
    mine_reads = readers_ref[me]
    slot = jnp.where(
        mine_reads == last_at,
        prefixes - 1,
        jnp.where(mine_reads > last_at, mine_reads - 1, mine_reads),
    )

    pl.semaphore_wait(barrier, replicas - 1)

    def rs_copy(t, part):
        b = orders[part][t]
        rows = part_rows >> (t + 1)
        low = range_low(me, part, t) + (1 - my_bits[b]) * rows
        if t == 0:
            src = prefix_ref.at[rows_at(low, rows), :]
            dst = first_recv.at[part]
        else:
            src = work.at[:, rows_at(low, rows), :]
            dst = later_recv.at[part, :, pl.ds((part_rows >> 1) - 2 * rows, rows), :]
        return pltpu.make_async_remote_copy(
            src_ref=src,
            dst_ref=dst,
            send_sem=rs_send.at[t, part],
            recv_sem=rs_recv.at[t, part],
            device_id={"replica": flip(1 << b)},
            device_id_type=MESH,
        )

    def rs_take(t, part):
        b = orders[part][t]
        rows = part_rows >> (t + 1)
        low = range_low(me, part, t) + my_bits[b] * rows
        for d in range(dynamic):
            other = bit_of(dynamic_owner[d], b) != my_bits[b]
            if t == 0:
                mine = prefix_ref[rows_at(low, rows), :]
                theirs = first_recv[part]
            else:
                mine = work[d, rows_at(low, rows), :]
                theirs = later_recv[part, d, pl.ds((part_rows >> 1) - 2 * rows, rows), :]
            chosen = jnp.where(other, theirs, mine)
            if t == steps - 1:
                gathered[d, rows_at(low, rows), :] = chosen
            else:
                work[d, rows_at(low, rows), :] = chosen

    def slots_of(fixed):
        return pl.ds(dynamic, 1) if fixed else pl.ds(0, dynamic)

    def ag_copy(t, part, fixed):
        b = orders[part][t]
        rows = part_rows >> (t + 1)
        view = gathered.at[slots_of(fixed), rows_at(range_low(me, part, t + 1), rows), :]
        return pltpu.make_async_remote_copy(
            src_ref=view,
            dst_ref=view,
            send_sem=ag_send.at[t, part, fixed],
            recv_sem=ag_recv.at[t, part, fixed],
            device_id={"replica": flip(1 << b)},
            device_id_type=MESH,
        )

    def quarter(device, part, taken):
        b = orders[part][1]
        side = bit_of(device, b) if taken == 0 else 1 - bit_of(device, b)
        return range_low(device, part, 1) + side * (part_rows >> 2)

    def core_copy(taken, part, fixed):
        view = gathered.at[
            slots_of(fixed), rows_at(quarter(me, part, taken), part_rows >> 2), :
        ]
        return pltpu.make_async_remote_copy(
            src_ref=view,
            dst_ref=view,
            send_sem=core_send.at[taken, part, fixed],
            recv_sem=core_recv.at[taken, part, fixed],
            device_id={"replica": flip(1)},
            device_id_type=MESH,
        )

    def scatter_copy(target, part):
        low = range_low(target, part, steps)
        return pltpu.make_async_remote_copy(
            src_ref=prefix_ref.at[rows_at(low, piece), :],
            dst_ref=gathered.at[prefixes - 1, rows_at(low, piece), :],
            send_sem=st_send.at[target, part],
            recv_sem=st_recv.at[part],
            device_id={"replica": target},
            device_id_type=MESH,
        )

    def move_copy(i):
        return pltpu.make_async_remote_copy(
            src_ref=out_blocks.at[i],
            dst_ref=arrived.at[i + 1],
            send_sem=mv_send.at[i],
            recv_sem=mv_recv.at[i],
            device_id={"replica": flip(order[i])},
            device_id_type=MESH,
        )

    def picked(target):
        code = codes[target, 0]
        block = pool_ref[jnp.maximum(code, 0)]
        return jnp.where(code >= 0, block, jnp.full_like(block, DEAD))

    issued = [0]

    def issue(n):
        for _ in range(n):
            i = issued[0]
            if i < replicas - 1:
                out_blocks[i] = picked(flip(order[i]))
                move_copy(i).start()
                issued[0] = i + 1

    for part in range(parts):
        rs_copy(0, part).start()

    @pl.when(me == replicas - 1)
    def _():
        def send(target, c):
            for part in range(parts):
                scatter_copy(target, part).start()
            return c

        lax.fori_loop(0, replicas - 1, send, 0)
        for part in range(parts):
            low = range_low(me, part, steps)
            gathered[prefixes - 1, rows_at(low, piece), :] = prefix_ref[rows_at(low, piece), :]

    code_copy.wait()
    issue(4)
    arrived[0] = picked(me)

    m_ref[...] = jnp.full_like(m_ref, -jnp.inf)
    l_ref[...] = jnp.zeros_like(l_ref)
    acc_ref[...] = jnp.zeros_like(acc_ref)

    def attend(load, mask_of=None):
        key_value = load()
        count = key_value.shape[0]
        mask = None if mask_of is None else mask_of()

        def one_head(h, c):
            q = q_ref[:, pl.ds(pl.multiple_of(h * hd, hd), hd)]
            scores = lax.dot_general(
                q, key_value[:, :hd], (((1,), (1,)), ((), ())), preferred_element_type=jnp.float32
            )
            if mask is not None:
                scores = jnp.where(mask, scores, -jnp.inf)
            before = m_ref[h]
            new_max = jnp.maximum(before, jnp.max(scores, axis=1, keepdims=True))
            shrink = jnp.exp2((before - new_max) * coef)
            total = l_ref[h] * shrink
            top = new_max * coef
            weights = []
            for g in range(count // hd):
                w = jnp.exp2(scores[:, g * hd : (g + 1) * hd] * coef - top)
                total = total + w
                weights.append(w.astype(jnp.bfloat16))
            l_ref[h] = total
            m_ref[h] = new_max
            acc_ref[h] = acc_ref[h] * shrink + jnp.dot(
                jnp.concatenate(weights, axis=1),
                key_value[:, hd:],
                preferred_element_type=jnp.float32,
            )
            return c

        lax.fori_loop(0, heads, one_head, 0, unroll=2)

    def attend_suffix():
        n = suffix_ref.shape[0]
        causal = lambda: (
            lax.broadcasted_iota(jnp.int32, (n, n), 1) <= lax.broadcasted_iota(jnp.int32, (n, n), 0)
        )
        attend(lambda: suffix_ref[...], causal)

    def attend_own():
        n = own_ref.shape[0]
        attend(
            lambda: own_ref[...],
            lambda: lax.broadcasted_iota(jnp.int32, (1, n), 1) < ctx_ref[0],
        )

    block = arrived.shape[1]
    chunk = 4
    groups = list(range(0, replicas, chunk))

    def attend_moved():
        if not groups:
            return
        first = groups.pop(0)
        for k in range(first, first + chunk):
            if k > 0:
                move_copy(k - 1).wait_recv()
        attend(
            lambda: arrived[pl.ds(first, chunk)].reshape(chunk * block, 2 * hd),
            lambda: jnp.concatenate(
                [
                    jnp.concatenate(
                        [arrived[k, 0:16, 0:hd].astype(jnp.float32)[0:1]] * (block // hd), axis=1
                    )
                    for k in range(first, first + chunk)
                ],
                axis=1,
            )
            < LIMIT,
        )

    def attend_prefix(low, rows):
        def load():
            key_value = gathered[0, rows_at(low, rows), :]
            for p in range(1, prefixes):
                key_value = jnp.where(slot == p, gathered[p, rows_at(low, rows), :], key_value)
            return key_value

        attend(load)

    def rs_step(t):
        for part in range(parts):
            rs_copy(t, part).wait()
            rs_take(t, part)
            if t + 1 < steps:
                rs_copy(t + 1, part).start()

    def scatter_wait():
        @pl.when(me != replicas - 1)
        def _():
            for part in range(parts):
                scatter_copy(me, part).wait_recv()

    def ag_begin(fixed):
        for part in range(parts):
            ag_copy(steps - 1, part, fixed).start()

    def ag_step(t, fixed):
        for part in range(parts):
            ag_copy(t, part, fixed).wait()
            if t > 1:
                ag_copy(t - 1, part, fixed).start()
            if t == 2:
                core_copy(0, part, fixed).start()
            if t == 1:
                core_copy(1, part, fixed).start()

    DYN, FIX = 0, 1
    events = []
    for t in range(steps):
        events.append(functools.partial(rs_step, t))
    events.append(lambda: ag_begin(DYN))
    for t in range(steps - 1, 1, -1):
        events.append(functools.partial(ag_step, t, DYN))
    fixed_events = [lambda: (scatter_wait(), ag_begin(FIX))]
    for t in range(steps - 1, 0, -1):
        fixed_events.append(functools.partial(ag_step, t, FIX))
    merged = events[: steps - 2]
    rest = events[steps - 2 :]
    while rest or fixed_events:
        if fixed_events:
            merged.append(fixed_events.pop(0))
        if rest:
            merged.append(rest.pop(0))
    fill = [None, attend_suffix, attend_own]
    for i, event in enumerate(merged):
        event()
        issue(2)
        if i < len(fill):
            if fill[i] is not None:
                fill[i]()
        elif groups[0] + chunk <= issued[0]:
            attend_moved()
    issue(replicas)
    quarter_rows = part_rows >> 2
    beside = flip(1)
    for part in range(parts):
        attend_prefix(quarter(me, part, 0), quarter_rows)
    for part in range(parts):
        for fixed in (DYN, FIX):
            core_copy(0, part, fixed).wait()
        attend_prefix(quarter(beside, part, 0), quarter_rows)
    ag_step(1, DYN)
    for part in range(parts):
        attend_prefix(quarter(me, part, 1), quarter_rows)
    for part in range(parts):
        for fixed in (DYN, FIX):
            core_copy(1, part, fixed).wait()
        attend_prefix(quarter(beside, part, 1), quarter_rows)
    while groups:
        attend_moved()

    for h in range(heads):
        denominator = jnp.sum(l_ref[h], axis=1, keepdims=True)
        o_ref[:, h * hd : (h + 1) * hd] = (acc_ref[h] / denominator).astype(o_ref.dtype)

    for i in range(replicas - 1):
        move_copy(i).wait_send()

    @pl.when(me == replicas - 1)
    def _():
        def done(target, c):
            for part in range(parts):
                scatter_copy(target, part).wait_send()
            return c

        lax.fori_loop(0, replicas - 1, done, 0)


def on_device(
    queries,
    suffix_kv,
    own_cache,
    ctx_len,
    prefix_cache,
    owners,
    readers,
    kv_pool,
    mig_target,
    mig_block,
    mig_count,
):
    replicas = lax.axis_size("replica")
    hd = suffix_kv.shape[1] // 2
    heads = queries.shape[1] // hd
    tokens = queries.shape[0]
    prefixes = owners.shape[0]
    steps = replicas.bit_length() - 1
    prefix_len, width = prefix_cache.shape
    part_rows = prefix_len // 2
    vmem = pl.BlockSpec(memory_space=pltpu.VMEM)
    smem = pl.BlockSpec(memory_space=pltpu.SMEM)
    dma = pltpu.SemaphoreType.DMA
    return pl.pallas_call(
        functools.partial(attention_kernel, (replicas, prefixes, heads, hd)),
        out_shape=jax.ShapeDtypeStruct(queries.shape, jnp.bfloat16),
        in_specs=[smem] * 4 + [vmem] * 7,
        out_specs=vmem,
        scratch_shapes=[
            pltpu.VMEM((prefixes, prefix_len, width), jnp.bfloat16),
            pltpu.VMEM((prefixes - 1, prefix_len, width), jnp.bfloat16),
            pltpu.VMEM((2, part_rows // 2, width), jnp.bfloat16),
            pltpu.VMEM((2, prefixes - 1, part_rows // 2, width), jnp.bfloat16),
            pltpu.VMEM((replicas,) + kv_pool.shape[1:], jnp.bfloat16),
            pltpu.VMEM((replicas,) + kv_pool.shape[1:], jnp.bfloat16),
            pltpu.VMEM((replicas, 128), jnp.int32),
            pltpu.SMEM((replicas, 128), jnp.int32),
            pltpu.VMEM((heads, tokens, hd), jnp.float32),
            pltpu.VMEM((heads, tokens, hd), jnp.float32),
            pltpu.VMEM((heads, tokens, hd), jnp.float32),
            dma((steps, 2)),
            dma((steps, 2)),
            dma((steps, 2, 2)),
            dma((steps, 2, 2)),
            dma((replicas, 2)),
            dma((2,)),
            dma((replicas,)),
            dma((replicas,)),
            dma((2, 2, 2)),
            dma((2, 2, 2)),
            dma,
        ],
        compiler_params=pltpu.CompilerParams(
            collective_id=0, has_side_effects=True, vmem_limit_bytes=56 * 1024 * 1024
        ),
    )(
        ctx_len,
        owners,
        readers,
        mig_count,
        mig_target,
        mig_block,
        queries,
        suffix_kv,
        own_cache,
        prefix_cache,
        kv_pool,
    )


def solution(mesh):
    in_specs = (
        P(("groups", "replica"), None),
        P(("groups", "replica"), None),
        P(("groups", "replica"), None),
        P(("groups", "replica")),
        P(("groups", "replica"), None),
        P("groups"),
        P("groups"),
        P(("groups", "replica"), None, None),
        P(("groups", "replica"), None),
        P(("groups", "replica"), None),
        P(("groups", "replica")),
    )
    out_specs = P(("groups", "replica"), None)
    return jax.shard_map(
        on_device, mesh=mesh, in_specs=in_specs, out_specs=out_specs, check_vma=False
    )
```

```python
import functools
import math

import jax
import jax.numpy as jnp
from jax import lax
from jax.experimental import pallas as pl
from jax.experimental.pallas import tpu as pltpu
from jax.sharding import PartitionSpec as P

DEAD = 64.0
LIMIT = 32.0
MESH = pl.DeviceIdType.MESH


def move_order(replicas):
    top = replicas // 2
    near = 8 if replicas >= 16 else 2

    def key(k):
        return (k % near < 2, k)

    across = sorted(range(top, replicas), key=key)
    within = sorted(range(1, top), key=key)
    order = []
    while across or within:
        if across:
            order.append(across.pop(0))
        if within:
            order.append(within.pop(0))
    return order


def attention_kernel(
    cfg,
    ctx_ref,
    owners_ref,
    readers_ref,
    count_ref,
    target_ref,
    block_ref,
    q_ref,
    suffix_ref,
    own_ref,
    prefix_ref,
    pool_ref,
    o_ref,
    gathered,
    work,
    first_recv,
    later_recv,
    arrived,
    out_blocks,
    codes_vmem,
    codes,
    q_rows,
    m_ref,
    l_ref,
    acc_ref,
    rs_send,
    rs_recv,
    ag_send,
    ag_recv,
    st_send,
    st_recv,
    mv_send,
    mv_recv,
    core_send,
    core_recv,
    code_sem,
):
    replicas, prefixes, heads, hd = cfg
    steps = replicas.bit_length() - 1
    prefix_len = prefix_ref.shape[0]
    parts = 2
    part_rows = prefix_len // parts
    piece = part_rows // replicas
    dynamic = prefixes - 1
    orders = [list(range(steps)), list(range(steps))]
    if steps > 2:
        orders[1][1], orders[1][2] = orders[1][2], orders[1][1]
    me = lax.axis_index("replica")
    coef = hd ** (-0.5) * math.log2(math.e)
    order = move_order(replicas)

    def bit_of(device, b):
        return lax.rem(device // (1 << b), 2)

    my_bits = [bit_of(me, b) for b in range(steps)]

    def flip(k):
        device = me
        for b in range(steps):
            if (k >> b) & 1:
                device = device + (1 - 2 * my_bits[b]) * (1 << b)
        return device

    def range_low(device, part, level):
        low = part * part_rows
        for t in range(level):
            low = low + bit_of(device, orders[part][t]) * (part_rows >> (t + 1))
        return low

    def rows_at(low, count):
        return pl.ds(pl.multiple_of(low, piece), count)

    barrier = pltpu.get_barrier_semaphore()

    def greet(i, c):
        pl.semaphore_signal(
            barrier, inc=1, device_id={"replica": lax.rem(me + i, replicas)}, device_id_type=MESH
        )
        return c

    lax.fori_loop(1, replicas, greet, 0)

    n_entries = target_ref.shape[1]
    shape = (replicas, n_entries)
    live = lax.broadcasted_iota(jnp.int32, shape, 1) < count_ref[0]
    hit = (target_ref[...] == lax.broadcasted_iota(jnp.int32, shape, 0)) & live
    found = jnp.sum(jnp.where(hit, block_ref[...] + 1, 0), axis=1, keepdims=True) - 1
    codes_vmem[...] = jnp.broadcast_to(found, codes_vmem.shape)
    code_copy = pltpu.make_async_copy(codes_vmem, codes, code_sem)
    code_copy.start()

    last_at = jnp.int32(0)
    for p in range(prefixes):
        last_at = jnp.where(owners_ref[p] == replicas - 1, p, last_at)
    dynamic_owner = []
    for d in range(dynamic):
        dynamic_owner.append(jnp.where(last_at <= d, owners_ref[d + 1], owners_ref[d]))
    mine_reads = readers_ref[me]
    slot = jnp.where(
        mine_reads == last_at,
        prefixes - 1,
        jnp.where(mine_reads > last_at, mine_reads - 1, mine_reads),
    )

    pl.semaphore_wait(barrier, replicas - 1)

    def rs_copy(t, part):
        b = orders[part][t]
        rows = part_rows >> (t + 1)
        low = range_low(me, part, t) + (1 - my_bits[b]) * rows
        if t == 0:
            src = prefix_ref.at[rows_at(low, rows), :]
            dst = first_recv.at[part]
        else:
            src = work.at[:, rows_at(low, rows), :]
            dst = later_recv.at[part, :, pl.ds((part_rows >> 1) - 2 * rows, rows), :]
        return pltpu.make_async_remote_copy(
            src_ref=src,
            dst_ref=dst,
            send_sem=rs_send.at[t, part],
            recv_sem=rs_recv.at[t, part],
            device_id={"replica": flip(1 << b)},
            device_id_type=MESH,
        )

    def rs_take(t, part):
        b = orders[part][t]
        rows = part_rows >> (t + 1)
        low = range_low(me, part, t) + my_bits[b] * rows
        for d in range(dynamic):
            other = bit_of(dynamic_owner[d], b) != my_bits[b]
            if t == 0:
                mine = prefix_ref[rows_at(low, rows), :]
                theirs = first_recv[part]
            else:
                mine = work[d, rows_at(low, rows), :]
                theirs = later_recv[part, d, pl.ds((part_rows >> 1) - 2 * rows, rows), :]
            chosen = jnp.where(other, theirs, mine)
            if t == steps - 1:
                gathered[d, rows_at(low, rows), :] = chosen
            else:
                work[d, rows_at(low, rows), :] = chosen

    def slots_of(fixed):
        return pl.ds(dynamic, 1) if fixed else pl.ds(0, dynamic)

    def ag_copy(t, part, fixed):
        b = orders[part][t]
        rows = part_rows >> (t + 1)
        view = gathered.at[slots_of(fixed), rows_at(range_low(me, part, t + 1), rows), :]
        return pltpu.make_async_remote_copy(
            src_ref=view,
            dst_ref=view,
            send_sem=ag_send.at[t, part, fixed],
            recv_sem=ag_recv.at[t, part, fixed],
            device_id={"replica": flip(1 << b)},
            device_id_type=MESH,
        )

    def quarter(device, part, taken):
        b = orders[part][1]
        side = bit_of(device, b) if taken == 0 else 1 - bit_of(device, b)
        return range_low(device, part, 1) + side * (part_rows >> 2)

    def core_copy(taken, part, fixed):
        view = gathered.at[
            slots_of(fixed), rows_at(quarter(me, part, taken), part_rows >> 2), :
        ]
        return pltpu.make_async_remote_copy(
            src_ref=view,
            dst_ref=view,
            send_sem=core_send.at[taken, part, fixed],
            recv_sem=core_recv.at[taken, part, fixed],
            device_id={"replica": flip(1)},
            device_id_type=MESH,
        )

    def scatter_copy(target, part):
        low = range_low(target, part, steps)
        return pltpu.make_async_remote_copy(
            src_ref=prefix_ref.at[rows_at(low, piece), :],
            dst_ref=gathered.at[prefixes - 1, rows_at(low, piece), :],
            send_sem=st_send.at[target, part],
            recv_sem=st_recv.at[part],
            device_id={"replica": target},
            device_id_type=MESH,
        )

    def move_copy(i):
        return pltpu.make_async_remote_copy(
            src_ref=out_blocks.at[i],
            dst_ref=arrived.at[i + 1],
            send_sem=mv_send.at[i],
            recv_sem=mv_recv.at[i],
            device_id={"replica": flip(order[i])},
            device_id_type=MESH,
        )

    def picked(target):
        code = codes[target, 0]
        block = pool_ref[jnp.maximum(code, 0)]
        return jnp.where(code >= 0, block, jnp.full_like(block, DEAD))

    issued = [0]

    def issue(n):
        for _ in range(n):
            i = issued[0]
            if i < replicas - 1:
                out_blocks[i] = picked(flip(order[i]))
                move_copy(i).start()
                issued[0] = i + 1

    for part in range(parts):
        rs_copy(0, part).start()

    @pl.when(me == replicas - 1)
    def _():
        def send(target, c):
            for part in range(parts):
                scatter_copy(target, part).start()
            return c

        lax.fori_loop(0, replicas - 1, send, 0)
        for part in range(parts):
            low = range_low(me, part, steps)
            gathered[prefixes - 1, rows_at(low, piece), :] = prefix_ref[rows_at(low, piece), :]

    code_copy.wait()
    issue(4)
    arrived[0] = picked(me)

    m_ref[...] = jnp.full_like(m_ref, -jnp.inf)
    l_ref[...] = jnp.zeros_like(l_ref)
    acc_ref[...] = jnp.zeros_like(acc_ref)

    tokens = q_ref.shape[0]
    for h in range(heads):
        q_rows[h * tokens : (h + 1) * tokens, :] = q_ref[:, h * hd : (h + 1) * hd]

    def attend(key_value, mask_scores=None):
        count = key_value.shape[0]
        scores = lax.dot_general(
            q_rows[...],
            key_value[:, :hd],
            (((1,), (1,)), ((), ())),
            preferred_element_type=jnp.float32,
        )
        if mask_scores is not None:
            scores = mask_scores(scores)
        before = m_ref[...]
        new_max = jnp.maximum(before, jnp.max(scores, axis=1, keepdims=True))
        shrink = jnp.exp2((before - new_max) * coef)
        total = l_ref[...] * shrink
        top = new_max * coef
        weights = []
        for g in range(count // hd):
            w = jnp.exp2(scores[:, g * hd : (g + 1) * hd] * coef - top)
            total = total + w
            weights.append(w.astype(jnp.bfloat16))
        l_ref[...] = total
        m_ref[...] = new_max
        acc_ref[...] = acc_ref[...] * shrink + jnp.dot(
            jnp.concatenate(weights, axis=1),
            key_value[:, hd:],
            preferred_element_type=jnp.float32,
        )

    unit = 256

    def attend_suffix():
        n = suffix_ref.shape[0]
        causal = lax.broadcasted_iota(jnp.int32, (tokens, n), 1) <= lax.broadcasted_iota(
            jnp.int32, (tokens, n), 0
        )

        def masked(scores):
            return jnp.concatenate(
                [
                    jnp.where(causal, scores[h * tokens : (h + 1) * tokens], -jnp.inf)
                    for h in range(heads)
                ],
                axis=0,
            )

        attend(suffix_ref[...], masked)

    def attend_own():
        def piece_of(j, c):
            low = pl.multiple_of(j * unit, unit)
            visible = lax.broadcasted_iota(jnp.int32, (1, unit), 1) < ctx_ref[0] - low
            attend(
                own_ref[pl.ds(low, unit), :],
                lambda scores: jnp.where(visible, scores, -jnp.inf),
            )
            return c

        lax.fori_loop(0, own_ref.shape[0] // unit, piece_of, 0)

    block = arrived.shape[1]
    chunk = unit // block
    groups = list(range(0, replicas, chunk))

    def attend_moved():
        first = groups.pop(0)
        for k in range(first, first + chunk):
            if k > 0:
                move_copy(k - 1).wait_recv()
        flags = jnp.concatenate(
            [
                arrived[k, 0:16, 0:hd].astype(jnp.float32)[0:1]
                for k in range(first, first + chunk)
                for _ in range(block // hd)
            ],
            axis=1,
        )
        attend(
            arrived[pl.ds(first, chunk)].reshape(unit, 2 * hd),
            lambda scores: jnp.where(flags < LIMIT, scores, -jnp.inf),
        )

    def attend_prefix(low, rows):
        def piece_of(j, c):
            start = low + j * unit
            key_value = gathered[0, rows_at(start, unit), :]
            for p in range(1, prefixes):
                key_value = jnp.where(slot == p, gathered[p, rows_at(start, unit), :], key_value)
            attend(key_value)
            return c

        lax.fori_loop(0, rows // unit, piece_of, 0)

    def rs_step(t):
        for part in range(parts):
            rs_copy(t, part).wait()
            rs_take(t, part)
            if t + 1 < steps:
                rs_copy(t + 1, part).start()

    def scatter_wait():
        @pl.when(me != replicas - 1)
        def _():
            for part in range(parts):
                scatter_copy(me, part).wait_recv()

    def ag_begin(fixed):
        for part in range(parts):
            ag_copy(steps - 1, part, fixed).start()

    def ag_step(t, fixed):
        for part in range(parts):
            ag_copy(t, part, fixed).wait()
            if t > 1:
                ag_copy(t - 1, part, fixed).start()
            if t == 2:
                core_copy(0, part, fixed).start()
            if t == 1:
                core_copy(1, part, fixed).start()

    DYN, FIX = 0, 1
    events = []
    for t in range(steps):
        events.append(functools.partial(rs_step, t))
    events.append(lambda: ag_begin(DYN))
    for t in range(steps - 1, 1, -1):
        events.append(functools.partial(ag_step, t, DYN))
    fixed_events = [lambda: (scatter_wait(), ag_begin(FIX))]
    for t in range(steps - 1, 0, -1):
        fixed_events.append(functools.partial(ag_step, t, FIX))
    merged = events[:3]
    rest = events[3:]
    while rest or fixed_events:
        if fixed_events:
            merged.append(fixed_events.pop(0))
        if rest:
            merged.append(rest.pop(0))
    fill = [None, attend_suffix, attend_own]
    for i, event in enumerate(merged):
        event()
        issue(2)
        if i < len(fill):
            if fill[i] is not None:
                fill[i]()
        else:
            for _ in range(1):
                if groups and groups[0] + chunk <= issued[0] - 2:
                    attend_moved()
    issue(replicas)
    quarter_rows = part_rows >> 2
    beside = flip(1)
    for part in range(parts):
        attend_prefix(quarter(me, part, 0), quarter_rows)
    for part in range(parts):
        for fixed in (DYN, FIX):
            core_copy(0, part, fixed).wait()
        attend_prefix(quarter(beside, part, 0), quarter_rows)
    ag_step(1, DYN)
    for part in range(parts):
        attend_prefix(quarter(me, part, 1), quarter_rows)
    for part in range(parts):
        for fixed in (DYN, FIX):
            core_copy(1, part, fixed).wait()
        attend_prefix(quarter(beside, part, 1), quarter_rows)
    while groups:
        attend_moved()

    for h in range(heads):
        rows = slice(h * tokens, (h + 1) * tokens)
        denominator = jnp.sum(l_ref[rows, :], axis=1, keepdims=True)
        o_ref[:, h * hd : (h + 1) * hd] = (acc_ref[rows, :] / denominator).astype(o_ref.dtype)

    for i in range(replicas - 1):
        move_copy(i).wait_send()

    @pl.when(me == replicas - 1)
    def _():
        def done(target, c):
            for part in range(parts):
                scatter_copy(target, part).wait_send()
            return c

        lax.fori_loop(0, replicas - 1, done, 0)


def on_device(
    queries,
    suffix_kv,
    own_cache,
    ctx_len,
    prefix_cache,
    owners,
    readers,
    kv_pool,
    mig_target,
    mig_block,
    mig_count,
):
    replicas = lax.axis_size("replica")
    hd = suffix_kv.shape[1] // 2
    heads = queries.shape[1] // hd
    tokens = queries.shape[0]
    prefixes = owners.shape[0]
    steps = replicas.bit_length() - 1
    prefix_len, width = prefix_cache.shape
    part_rows = prefix_len // 2
    vmem = pl.BlockSpec(memory_space=pltpu.VMEM)
    smem = pl.BlockSpec(memory_space=pltpu.SMEM)
    dma = pltpu.SemaphoreType.DMA
    return pl.pallas_call(
        functools.partial(attention_kernel, (replicas, prefixes, heads, hd)),
        out_shape=jax.ShapeDtypeStruct(queries.shape, jnp.bfloat16),
        in_specs=[smem] * 4 + [vmem] * 7,
        out_specs=vmem,
        scratch_shapes=[
            pltpu.VMEM((prefixes, prefix_len, width), jnp.bfloat16),
            pltpu.VMEM((prefixes - 1, prefix_len, width), jnp.bfloat16),
            pltpu.VMEM((2, part_rows // 2, width), jnp.bfloat16),
            pltpu.VMEM((2, prefixes - 1, part_rows // 2, width), jnp.bfloat16),
            pltpu.VMEM((replicas,) + kv_pool.shape[1:], jnp.bfloat16),
            pltpu.VMEM((replicas,) + kv_pool.shape[1:], jnp.bfloat16),
            pltpu.VMEM((replicas, 128), jnp.int32),
            pltpu.SMEM((replicas, 128), jnp.int32),
            pltpu.VMEM((heads * tokens, hd), jnp.bfloat16),
            pltpu.VMEM((heads * tokens, hd), jnp.float32),
            pltpu.VMEM((heads * tokens, hd), jnp.float32),
            pltpu.VMEM((heads * tokens, hd), jnp.float32),
            dma((steps, 2)),
            dma((steps, 2)),
            dma((steps, 2, 2)),
            dma((steps, 2, 2)),
            dma((replicas, 2)),
            dma((2,)),
            dma((replicas,)),
            dma((replicas,)),
            dma((2, 2, 2)),
            dma((2, 2, 2)),
            dma,
        ],
        compiler_params=pltpu.CompilerParams(
            collective_id=0, has_side_effects=True, vmem_limit_bytes=56 * 1024 * 1024
        ),
    )(
        ctx_len,
        owners,
        readers,
        mig_count,
        mig_target,
        mig_block,
        queries,
        suffix_kv,
        own_cache,
        prefix_cache,
        kv_pool,
    )


def solution(mesh):
    in_specs = (
        P(("groups", "replica"), None),
        P(("groups", "replica"), None),
        P(("groups", "replica"), None),
        P(("groups", "replica")),
        P(("groups", "replica"), None),
        P("groups"),
        P("groups"),
        P(("groups", "replica"), None, None),
        P(("groups", "replica"), None),
        P(("groups", "replica"), None),
        P(("groups", "replica")),
    )
    out_specs = P(("groups", "replica"), None)
    return jax.shard_map(
        on_device, mesh=mesh, in_specs=in_specs, out_specs=out_specs, check_vma=False
    )
```

```python
import functools
import math

import jax
import jax.numpy as jnp
from jax import lax
from jax.experimental import pallas as pl
from jax.experimental.pallas import tpu as pltpu
from jax.sharding import PartitionSpec as P

DEAD = 64.0
LIMIT = 32.0
MESH = pl.DeviceIdType.MESH


def move_order(replicas):
    top = replicas // 2
    near = 8 if replicas >= 16 else 2

    def key(k):
        return (k % near < 2, k)

    across = sorted(range(top, replicas), key=key)
    within = sorted(range(1, top), key=key)
    order = []
    while across or within:
        if across:
            order.append(across.pop(0))
        if within:
            order.append(within.pop(0))
    return order


def attention_kernel(
    cfg,
    ctx_ref,
    owners_ref,
    readers_ref,
    count_ref,
    target_ref,
    block_ref,
    q_ref,
    suffix_ref,
    own_ref,
    prefix_hbm,
    pool_hbm,
    o_ref,
    prefix_ref,
    pool_ref,
    gathered,
    work,
    first_recv,
    later_recv,
    arrived,
    out_blocks,
    codes_vmem,
    codes,
    q_rows,
    m_ref,
    l_ref,
    acc_ref,
    rs_send,
    rs_recv,
    ag_send,
    ag_recv,
    st_send,
    st_recv,
    mv_send,
    mv_recv,
    core_send,
    core_recv,
    code_sem,
    load_sem,
    half_send,
    half_recv,
    eighth_send,
    eighth_recv,
):
    replicas, prefixes, heads, hd = cfg
    steps = replicas.bit_length() - 1
    prefix_len = prefix_hbm.shape[0]
    parts = 2
    part_rows = prefix_len // parts
    piece = part_rows // replicas
    dynamic = prefixes - 1
    orders = [list(range(steps)), list(range(steps))]
    if steps > 2:
        orders[1][1], orders[1][2] = orders[1][2], orders[1][1]
    me = lax.axis_index("replica")
    coef = hd ** (-0.5) * math.log2(math.e)
    order = move_order(replicas)

    def bit_of(device, b):
        return lax.rem(device // (1 << b), 2)

    my_bits = [bit_of(me, b) for b in range(steps)]

    def flip(k):
        device = me
        for b in range(steps):
            if (k >> b) & 1:
                device = device + (1 - 2 * my_bits[b]) * (1 << b)
        return device

    def range_low(device, part, level):
        low = part * part_rows
        for t in range(level):
            low = low + bit_of(device, orders[part][t]) * (part_rows >> (t + 1))
        return low

    def rows_at(low, count):
        return pl.ds(pl.multiple_of(low, piece), count)

    load_pool = pltpu.make_async_copy(pool_hbm, pool_ref, load_sem.at[0])
    load_pool.start()
    load_prefix = pltpu.make_async_copy(prefix_hbm, prefix_ref, load_sem.at[1])
    load_prefix.start()
    barrier = pltpu.get_barrier_semaphore()

    def greet(i, c):
        pl.semaphore_signal(
            barrier, inc=1, device_id={"replica": lax.rem(me + i, replicas)}, device_id_type=MESH
        )
        return c

    lax.fori_loop(1, replicas, greet, 0)

    n_entries = target_ref.shape[1]
    shape = (replicas, n_entries)
    live = lax.broadcasted_iota(jnp.int32, shape, 1) < count_ref[0]
    hit = (target_ref[...] == lax.broadcasted_iota(jnp.int32, shape, 0)) & live
    found = jnp.sum(jnp.where(hit, block_ref[...] + 1, 0), axis=1, keepdims=True) - 1
    codes_vmem[...] = jnp.broadcast_to(found, codes_vmem.shape)
    code_copy = pltpu.make_async_copy(codes_vmem, codes, code_sem)
    code_copy.start()

    last_at = jnp.int32(0)
    for p in range(prefixes):
        last_at = jnp.where(owners_ref[p] == replicas - 1, p, last_at)
    dynamic_owner = []
    for d in range(dynamic):
        dynamic_owner.append(jnp.where(last_at <= d, owners_ref[d + 1], owners_ref[d]))
    mine_reads = readers_ref[me]
    slot = jnp.where(
        mine_reads == last_at,
        prefixes - 1,
        jnp.where(mine_reads > last_at, mine_reads - 1, mine_reads),
    )

    pl.semaphore_wait(barrier, replicas - 1)

    def rs_copy(t, part):
        b = orders[part][t]
        rows = part_rows >> (t + 1)
        low = range_low(me, part, t) + (1 - my_bits[b]) * rows
        if t == 0:
            src = prefix_hbm.at[rows_at(low, rows), :]
            dst = first_recv.at[part]
        else:
            src = work.at[:, rows_at(low, rows), :]
            dst = later_recv.at[part, :, pl.ds((part_rows >> 1) - 2 * rows, rows), :]
        return pltpu.make_async_remote_copy(
            src_ref=src,
            dst_ref=dst,
            send_sem=rs_send.at[t, part],
            recv_sem=rs_recv.at[t, part],
            device_id={"replica": flip(1 << b)},
            device_id_type=MESH,
        )

    def rs_take(t, part):
        b = orders[part][t]
        rows = part_rows >> (t + 1)
        low = range_low(me, part, t) + my_bits[b] * rows
        for d in range(dynamic):
            other = bit_of(dynamic_owner[d], b) != my_bits[b]
            if t == 0:
                mine = prefix_ref[rows_at(low, rows), :]
                theirs = first_recv[part]
            else:
                mine = work[d, rows_at(low, rows), :]
                theirs = later_recv[part, d, pl.ds((part_rows >> 1) - 2 * rows, rows), :]
            chosen = jnp.where(other, theirs, mine)
            if t == steps - 1:
                gathered[d, rows_at(low, rows), :] = chosen
            else:
                work[d, rows_at(low, rows), :] = chosen

    def slots_of(fixed):
        return pl.ds(dynamic, 1) if fixed else pl.ds(0, dynamic)

    def ag_copy(t, part, fixed):
        b = orders[part][t]
        rows = part_rows >> (t + 1)
        view = gathered.at[slots_of(fixed), rows_at(range_low(me, part, t + 1), rows), :]
        return pltpu.make_async_remote_copy(
            src_ref=view,
            dst_ref=view,
            send_sem=ag_send.at[t, part, fixed],
            recv_sem=ag_recv.at[t, part, fixed],
            device_id={"replica": flip(1 << b)},
            device_id_type=MESH,
        )

    def quarter(device, part, taken):
        b = orders[part][1]
        side = bit_of(device, b) if taken == 0 else 1 - bit_of(device, b)
        return range_low(device, part, 1) + side * (part_rows >> 2)

    def eighth(device, part, taken):
        b = orders[part][2]
        side = bit_of(device, b) if taken == 0 else 1 - bit_of(device, b)
        return range_low(device, part, 2) + side * (part_rows >> 3)

    def eighth_copy(taken, part, fixed):
        view = gathered.at[slots_of(fixed), rows_at(eighth(me, part, taken), part_rows >> 3), :]
        return pltpu.make_async_remote_copy(
            src_ref=view,
            dst_ref=view,
            send_sem=eighth_send.at[taken, part, fixed],
            recv_sem=eighth_recv.at[taken, part, fixed],
            device_id={"replica": flip(1)},
            device_id_type=MESH,
        )

    def core_copy(taken, part, fixed):
        view = gathered.at[
            slots_of(fixed), rows_at(quarter(me, part, taken), part_rows >> 2), :
        ]
        return pltpu.make_async_remote_copy(
            src_ref=view,
            dst_ref=view,
            send_sem=core_send.at[taken, part, fixed],
            recv_sem=core_recv.at[taken, part, fixed],
            device_id={"replica": flip(1)},
            device_id_type=MESH,
        )

    def half_copy(half, part, beyond):
        rows = part_rows >> 3
        low = quarter(me, part, 0 if beyond else 1) + half * rows
        view = gathered.at[slots_of(0), rows_at(low, rows), :]
        return pltpu.make_async_remote_copy(
            src_ref=view,
            dst_ref=view,
            send_sem=half_send.at[half, part, beyond],
            recv_sem=half_recv.at[half, part, beyond],
            device_id={"replica": flip(1 << orders[part][1]) if beyond else flip(1)},
            device_id_type=MESH,
        )

    def scatter_copy(target, part):
        low = range_low(target, part, steps)
        return pltpu.make_async_remote_copy(
            src_ref=prefix_hbm.at[rows_at(low, piece), :],
            dst_ref=gathered.at[prefixes - 1, rows_at(low, piece), :],
            send_sem=st_send.at[target, part],
            recv_sem=st_recv.at[part],
            device_id={"replica": target},
            device_id_type=MESH,
        )

    def move_copy(i):
        return pltpu.make_async_remote_copy(
            src_ref=out_blocks.at[i],
            dst_ref=arrived.at[i + 1],
            send_sem=mv_send.at[i],
            recv_sem=mv_recv.at[i],
            device_id={"replica": flip(order[i])},
            device_id_type=MESH,
        )

    def picked(target):
        code = codes[target, 0]
        block = pool_ref[jnp.maximum(code, 0)]
        return jnp.where(code >= 0, block, jnp.full_like(block, DEAD))

    issued = [0]

    def issue(n):
        for _ in range(n):
            i = issued[0]
            if i < replicas - 1:
                out_blocks[i] = picked(flip(order[i]))
                move_copy(i).start()
                issued[0] = i + 1

    for part in range(parts):
        rs_copy(0, part).start()

    load_pool.wait()
    load_prefix.wait()

    @pl.when(me == replicas - 1)
    def _():
        def send(target, c):
            for part in range(parts):
                scatter_copy(target, part).start()
            return c

        lax.fori_loop(0, replicas - 1, send, 0)
        for part in range(parts):
            low = range_low(me, part, steps)
            gathered[prefixes - 1, rows_at(low, piece), :] = prefix_ref[rows_at(low, piece), :]

    code_copy.wait()
    issue(4)
    arrived[0] = picked(me)

    m_ref[...] = jnp.full_like(m_ref, -jnp.inf)
    l_ref[...] = jnp.zeros_like(l_ref)
    acc_ref[...] = jnp.zeros_like(acc_ref)

    tokens = q_ref.shape[0]
    for h in range(heads):
        q_rows[h * tokens : (h + 1) * tokens, :] = q_ref[:, h * hd : (h + 1) * hd]

    def attend(key_value, mask_scores=None):
        count = key_value.shape[0]
        scores = lax.dot_general(
            q_rows[...],
            key_value[:, :hd],
            (((1,), (1,)), ((), ())),
            preferred_element_type=jnp.float32,
        )
        if mask_scores is not None:
            scores = mask_scores(scores)
        before = m_ref[...]
        new_max = jnp.maximum(before, jnp.max(scores, axis=1, keepdims=True))
        shrink = jnp.exp2((before - new_max) * coef)
        total = l_ref[...] * shrink
        top = new_max * coef
        weights = []
        for g in range(count // hd):
            w = jnp.exp2(scores[:, g * hd : (g + 1) * hd] * coef - top)
            total = total + w
            weights.append(w.astype(jnp.bfloat16))
        l_ref[...] = total
        m_ref[...] = new_max
        acc_ref[...] = acc_ref[...] * shrink + jnp.dot(
            jnp.concatenate(weights, axis=1),
            key_value[:, hd:],
            preferred_element_type=jnp.float32,
        )

    unit = 256

    def attend_suffix():
        n = suffix_ref.shape[0]
        causal = lax.broadcasted_iota(jnp.int32, (tokens, n), 1) <= lax.broadcasted_iota(
            jnp.int32, (tokens, n), 0
        )

        def masked(scores):
            return jnp.concatenate(
                [
                    jnp.where(causal, scores[h * tokens : (h + 1) * tokens], -jnp.inf)
                    for h in range(heads)
                ],
                axis=0,
            )

        attend(suffix_ref[...], masked)

    def attend_own():
        def piece_of(j, c):
            low = j * unit
            visible = lax.broadcasted_iota(jnp.int32, (1, unit), 1) < ctx_ref[0] - low
            attend(
                own_ref[pl.ds(low, unit), :],
                lambda scores: jnp.where(visible, scores, -jnp.inf),
            )
            return c

        for j in range(own_ref.shape[0] // unit):
            piece_of(j, 0)

    block = arrived.shape[1]
    chunk = unit // block
    groups = list(range(0, replicas, chunk))

    def attend_moved(n):
        n = min(n, len(groups))
        if n == 0:
            return
        first = groups[0]
        del groups[:n]
        for k in range(first, first + n * chunk):
            if k > 0:
                move_copy(k - 1).wait_recv()

        def group(j, c):
            low = first + j * chunk
            flags = jnp.concatenate(
                [
                    arrived[low + k, 0:16, 0:hd].astype(jnp.float32)[0:1]
                    for k in range(chunk)
                    for _ in range(block // hd)
                ],
                axis=1,
            )
            attend(
                arrived[pl.ds(low, chunk)].reshape(unit, 2 * hd),
                lambda scores: jnp.where(flags < LIMIT, scores, -jnp.inf),
            )
            return c

        for j in range(n):
            group(j, 0)

    def attend_prefix(lows):
        for low in lows:
            key_value = gathered[0, rows_at(low, unit), :]
            for p in range(1, prefixes):
                key_value = jnp.where(slot == p, gathered[p, rows_at(low, unit), :], key_value)
            attend(key_value)

    def rs_step(t):
        for part in range(parts):
            rs_copy(t, part).wait()
            rs_take(t, part)
            if t + 1 < steps:
                rs_copy(t + 1, part).start()

    def scatter_wait():
        @pl.when(me != replicas - 1)
        def _():
            for part in range(parts):
                scatter_copy(me, part).wait_recv()

    def ag_begin(fixed):
        for part in range(parts):
            ag_copy(steps - 1, part, fixed).start()

    def ag_step(t, fixed):
        for part in range(parts):
            ag_copy(t, part, fixed).wait()
            if t == 2 and not fixed:
                for half in range(2):
                    half_copy(half, part, 1).start()
            elif t > 1:
                ag_copy(t - 1, part, fixed).start()
            if t == 3 or t == 2:
                eighth_copy(3 - t, part, fixed).start()
            if t == 1:
                core_copy(1, part, fixed).start()

    DYN, FIX = 0, 1
    both = range(parts)
    beside = flip(1)

    def attend_eighths(device, taken):
        if device is not me:
            for part in both:
                for fixed in (DYN, FIX):
                    eighth_copy(taken, part, fixed).wait()
        attend_prefix([eighth(device, part, taken) for part in both])

    step = functools.partial
    merged = [step(rs_step, t) for t in range(steps - 2)]
    merged += [lambda: (scatter_wait(), ag_begin(FIX)), step(rs_step, steps - 2)]
    merged += [step(ag_step, steps - 1, FIX), lambda: (rs_step(steps - 1), ag_begin(DYN))]
    for t in range(steps - 1, 1, -1):
        merged += [step(ag_step, t - 1, FIX), step(ag_step, t, DYN)]
    last = len(merged) - 1
    moved_at = {3: 1, 4: 1, 5: 1, 6: 1, 7: 2, 8: 1, 9: 2, 11: 2}
    for i, event in enumerate(merged):
        event()
        issue(2)
        if i == 1:
            attend_suffix()
        elif i == 2:
            attend_own()
        attend_moved(moved_at.get(i, 0))
        if i == last - 2:
            attend_eighths(me, 0)
        elif i == last - 1:
            attend_eighths(beside, 0)
    issue(replicas)
    half_rows = part_rows >> 3
    attend_eighths(me, 1)
    attend_eighths(beside, 1)
    attend_moved(len(groups) - 2)
    for part in both:
        core_copy(1, part, FIX).wait()
    for half in range(2):
        for part in both:
            half_copy(half, part, 1).wait()
            half_copy(half, part, 0).start()
        if half == 1:
            attend_moved(2)
        attend_prefix([quarter(me, part, 1) + half * half_rows for part in both])
        for part in both:
            half_copy(half, part, 0).wait()
        attend_prefix([quarter(beside, part, 1) + half * half_rows for part in both])

    for h in range(heads):
        rows = slice(h * tokens, (h + 1) * tokens)
        denominator = jnp.sum(l_ref[rows, :], axis=1, keepdims=True)
        o_ref[:, h * hd : (h + 1) * hd] = (acc_ref[rows, :] / denominator).astype(o_ref.dtype)

    for i in range(replicas - 1):
        move_copy(i).wait_send()

    @pl.when(me == replicas - 1)
    def _():
        def done(target, c):
            for part in range(parts):
                scatter_copy(target, part).wait_send()
            return c

        lax.fori_loop(0, replicas - 1, done, 0)


def on_device(
    queries,
    suffix_kv,
    own_cache,
    ctx_len,
    prefix_cache,
    owners,
    readers,
    kv_pool,
    mig_target,
    mig_block,
    mig_count,
):
    replicas = lax.axis_size("replica")
    hd = suffix_kv.shape[1] // 2
    heads = queries.shape[1] // hd
    tokens = queries.shape[0]
    prefixes = owners.shape[0]
    steps = replicas.bit_length() - 1
    prefix_len, width = prefix_cache.shape
    part_rows = prefix_len // 2
    vmem = pl.BlockSpec(memory_space=pltpu.VMEM)
    smem = pl.BlockSpec(memory_space=pltpu.SMEM)
    dma = pltpu.SemaphoreType.DMA
    return pl.pallas_call(
        functools.partial(attention_kernel, (replicas, prefixes, heads, hd)),
        out_shape=jax.ShapeDtypeStruct(queries.shape, jnp.bfloat16),
        in_specs=[smem] * 4 + [vmem] * 5 + [pl.BlockSpec(memory_space=pl.ANY)] * 2,
        out_specs=vmem,
        scratch_shapes=[
            pltpu.VMEM(prefix_cache.shape, jnp.bfloat16),
            pltpu.VMEM(kv_pool.shape, jnp.bfloat16),
            pltpu.VMEM((prefixes, prefix_len, width), jnp.bfloat16),
            pltpu.VMEM((prefixes - 1, prefix_len, width), jnp.bfloat16),
            pltpu.VMEM((2, part_rows // 2, width), jnp.bfloat16),
            pltpu.VMEM((2, prefixes - 1, part_rows // 2, width), jnp.bfloat16),
            pltpu.VMEM((replicas,) + kv_pool.shape[1:], jnp.bfloat16),
            pltpu.VMEM((replicas,) + kv_pool.shape[1:], jnp.bfloat16),
            pltpu.VMEM((replicas, 128), jnp.int32),
            pltpu.SMEM((replicas, 128), jnp.int32),
            pltpu.VMEM((heads * tokens, hd), jnp.bfloat16),
            pltpu.VMEM((heads * tokens, hd), jnp.float32),
            pltpu.VMEM((heads * tokens, hd), jnp.float32),
            pltpu.VMEM((heads * tokens, hd), jnp.float32),
            dma((steps, 2)),
            dma((steps, 2)),
            dma((steps, 2, 2)),
            dma((steps, 2, 2)),
            dma((replicas, 2)),
            dma((2,)),
            dma((replicas,)),
            dma((replicas,)),
            dma((2, 2, 2)),
            dma((2, 2, 2)),
            dma,
            dma((2,)),
            dma((2, 2, 2)),
            dma((2, 2, 2)),
            dma((2, 2, 2)),
            dma((2, 2, 2)),
        ],
        compiler_params=pltpu.CompilerParams(
            collective_id=0, has_side_effects=True, vmem_limit_bytes=56 * 1024 * 1024
        ),
    )(
        ctx_len,
        owners,
        readers,
        mig_count,
        mig_target,
        mig_block,
        queries,
        suffix_kv,
        own_cache,
        prefix_cache,
        kv_pool,
    )


def solution(mesh):
    in_specs = (
        P(("groups", "replica"), None),
        P(("groups", "replica"), None),
        P(("groups", "replica"), None),
        P(("groups", "replica")),
        P(("groups", "replica"), None),
        P("groups"),
        P("groups"),
        P(("groups", "replica"), None, None),
        P(("groups", "replica"), None),
        P(("groups", "replica"), None),
        P(("groups", "replica")),
    )
    out_specs = P(("groups", "replica"), None)
    return jax.shard_map(
        on_device, mesh=mesh, in_specs=in_specs, out_specs=out_specs, check_vma=False
    )
```

```python
import functools
import math

import jax
import jax.numpy as jnp
from jax import lax
from jax.experimental import pallas as pl
from jax.experimental.pallas import tpu as pltpu
from jax.sharding import PartitionSpec as P

DEAD = 64.0
LIMIT = 32.0
MESH = pl.DeviceIdType.MESH


def move_order(replicas):
    top = replicas // 2
    near = 8 if replicas >= 16 else 2

    def key(k):
        return (k % near < 2, k)

    across = sorted(range(top, replicas), key=key)
    within = sorted(range(1, top), key=key)
    order = []
    while across or within:
        if within:
            order.append(within.pop(0))
        if across:
            order.append(across.pop(0))
    return order


def attention_kernel(
    cfg,
    ctx_ref,
    owners_ref,
    readers_ref,
    count_ref,
    target_ref,
    block_ref,
    q_ref,
    suffix_ref,
    own_ref,
    prefix_hbm,
    pool_hbm,
    o_ref,
    prefix_ref,
    pool_ref,
    gathered,
    work,
    first_recv,
    later_recv,
    arrived,
    out_blocks,
    codes_vmem,
    codes,
    q_rows,
    m_ref,
    l_ref,
    acc_ref,
    rs_send,
    rs_recv,
    ag_send,
    ag_recv,
    st_send,
    st_recv,
    mv_send,
    mv_recv,
    core_send,
    core_recv,
    code_sem,
    load_sem,
    half_send,
    half_recv,
    eighth_send,
    eighth_recv,
):
    replicas, prefixes, heads, hd = cfg
    steps = replicas.bit_length() - 1
    prefix_len = prefix_hbm.shape[0]
    parts = 2
    part_rows = prefix_len // parts
    piece = part_rows // replicas
    dynamic = prefixes - 1
    orders = [list(range(steps)), list(range(steps))]
    if steps > 2:
        orders[1][1], orders[1][2] = orders[1][2], orders[1][1]
    me = lax.axis_index("replica")
    coef = hd ** (-0.5) * math.log2(math.e)
    order = move_order(replicas)

    def bit_of(device, b):
        return lax.rem(device // (1 << b), 2)

    my_bits = [bit_of(me, b) for b in range(steps)]

    def flip(k):
        device = me
        for b in range(steps):
            if (k >> b) & 1:
                device = device + (1 - 2 * my_bits[b]) * (1 << b)
        return device

    def range_low(device, part, level):
        low = part * part_rows
        for t in range(level):
            low = low + bit_of(device, orders[part][t]) * (part_rows >> (t + 1))
        return low

    def rows_at(low, count):
        return pl.ds(pl.multiple_of(low, piece), count)

    load_pool = pltpu.make_async_copy(pool_hbm, pool_ref, load_sem.at[0])
    load_pool.start()
    load_prefix = pltpu.make_async_copy(prefix_hbm, prefix_ref, load_sem.at[1])
    load_prefix.start()
    barrier = pltpu.get_barrier_semaphore()

    def greet(i, c):
        pl.semaphore_signal(
            barrier, inc=1, device_id={"replica": lax.rem(me + i, replicas)}, device_id_type=MESH
        )
        return c

    lax.fori_loop(1, replicas, greet, 0)

    n_entries = target_ref.shape[1]
    shape = (replicas, n_entries)
    live = lax.broadcasted_iota(jnp.int32, shape, 1) < count_ref[0]
    hit = (target_ref[...] == lax.broadcasted_iota(jnp.int32, shape, 0)) & live
    found = jnp.sum(jnp.where(hit, block_ref[...] + 1, 0), axis=1, keepdims=True) - 1
    codes_vmem[...] = jnp.broadcast_to(found, codes_vmem.shape)
    code_copy = pltpu.make_async_copy(codes_vmem, codes, code_sem)
    code_copy.start()

    last_at = jnp.int32(0)
    for p in range(prefixes):
        last_at = jnp.where(owners_ref[p] == replicas - 1, p, last_at)
    dynamic_owner = []
    for d in range(dynamic):
        dynamic_owner.append(jnp.where(last_at <= d, owners_ref[d + 1], owners_ref[d]))
    mine_reads = readers_ref[me]
    slot = jnp.where(
        mine_reads == last_at,
        prefixes - 1,
        jnp.where(mine_reads > last_at, mine_reads - 1, mine_reads),
    )

    pl.semaphore_wait(barrier, replicas - 1)

    def rs_copy(t, part):
        b = orders[part][t]
        rows = part_rows >> (t + 1)
        low = range_low(me, part, t) + (1 - my_bits[b]) * rows
        if t == 0:
            src = prefix_hbm.at[rows_at(low, rows), :]
            dst = first_recv.at[part]
        else:
            src = work.at[:, rows_at(low, rows), :]
            dst = later_recv.at[part, :, pl.ds((part_rows >> 1) - 2 * rows, rows), :]
        return pltpu.make_async_remote_copy(
            src_ref=src,
            dst_ref=dst,
            send_sem=rs_send.at[t, part],
            recv_sem=rs_recv.at[t, part],
            device_id={"replica": flip(1 << b)},
            device_id_type=MESH,
        )

    def rs_take(t, part):
        b = orders[part][t]
        rows = part_rows >> (t + 1)
        low = range_low(me, part, t) + my_bits[b] * rows
        for d in range(dynamic):
            other = bit_of(dynamic_owner[d], b) != my_bits[b]
            if t == 0:
                mine = prefix_ref[rows_at(low, rows), :]
                theirs = first_recv[part]
            else:
                mine = work[d, rows_at(low, rows), :]
                theirs = later_recv[part, d, pl.ds((part_rows >> 1) - 2 * rows, rows), :]
            chosen = jnp.where(other, theirs, mine)
            if t == steps - 1:
                gathered[d, rows_at(low, rows), :] = chosen
            else:
                work[d, rows_at(low, rows), :] = chosen

    def slots_of(fixed):
        return pl.ds(dynamic, 1) if fixed else pl.ds(0, dynamic)

    def ag_copy(t, part, fixed):
        b = orders[part][t]
        rows = part_rows >> (t + 1)
        view = gathered.at[slots_of(fixed), rows_at(range_low(me, part, t + 1), rows), :]
        return pltpu.make_async_remote_copy(
            src_ref=view,
            dst_ref=view,
            send_sem=ag_send.at[t, part, fixed],
            recv_sem=ag_recv.at[t, part, fixed],
            device_id={"replica": flip(1 << b)},
            device_id_type=MESH,
        )

    def quarter(device, part, taken):
        b = orders[part][1]
        side = bit_of(device, b) if taken == 0 else 1 - bit_of(device, b)
        return range_low(device, part, 1) + side * (part_rows >> 2)

    def eighth(device, part, taken):
        b = orders[part][2]
        side = bit_of(device, b) if taken == 0 else 1 - bit_of(device, b)
        return range_low(device, part, 2) + side * (part_rows >> 3)

    def eighth_copy(taken, part, fixed):
        view = gathered.at[slots_of(fixed), rows_at(eighth(me, part, taken), part_rows >> 3), :]
        return pltpu.make_async_remote_copy(
            src_ref=view,
            dst_ref=view,
            send_sem=eighth_send.at[taken, part, fixed],
            recv_sem=eighth_recv.at[taken, part, fixed],
            device_id={"replica": flip(1)},
            device_id_type=MESH,
        )

    def core_copy(taken, part, fixed):
        view = gathered.at[
            slots_of(fixed), rows_at(quarter(me, part, taken), part_rows >> 2), :
        ]
        return pltpu.make_async_remote_copy(
            src_ref=view,
            dst_ref=view,
            send_sem=core_send.at[taken, part, fixed],
            recv_sem=core_recv.at[taken, part, fixed],
            device_id={"replica": flip(1)},
            device_id_type=MESH,
        )

    def half_copy(half, part, beyond):
        rows = part_rows >> 3
        low = quarter(me, part, 0 if beyond else 1) + half * rows
        view = gathered.at[slots_of(0), rows_at(low, rows), :]
        return pltpu.make_async_remote_copy(
            src_ref=view,
            dst_ref=view,
            send_sem=half_send.at[half, part, beyond],
            recv_sem=half_recv.at[half, part, beyond],
            device_id={"replica": flip(1 << orders[part][1]) if beyond else flip(1)},
            device_id_type=MESH,
        )

    def scatter_copy(target, part):
        low = range_low(target, part, steps)
        return pltpu.make_async_remote_copy(
            src_ref=prefix_hbm.at[rows_at(low, piece), :],
            dst_ref=gathered.at[prefixes - 1, rows_at(low, piece), :],
            send_sem=st_send.at[target, part],
            recv_sem=st_recv.at[part],
            device_id={"replica": target},
            device_id_type=MESH,
        )

    def move_copy(i):
        return pltpu.make_async_remote_copy(
            src_ref=out_blocks.at[i],
            dst_ref=arrived.at[i + 1],
            send_sem=mv_send.at[i],
            recv_sem=mv_recv.at[i],
            device_id={"replica": flip(order[i])},
            device_id_type=MESH,
        )

    def picked(target):
        code = codes[target, 0]
        block = pool_ref[jnp.maximum(code, 0)]
        return jnp.where(code >= 0, block, jnp.full_like(block, DEAD))

    issued = [0]

    def issue(n):
        for _ in range(n):
            i = issued[0]
            if i < replicas - 1:
                out_blocks[i] = picked(flip(order[i]))
                move_copy(i).start()
                issued[0] = i + 1

    for part in range(parts):
        rs_copy(0, part).start()

    load_pool.wait()
    load_prefix.wait()

    @pl.when(me == replicas - 1)
    def _():
        def send(target, c):
            for part in range(parts):
                scatter_copy(target, part).start()
            return c

        lax.fori_loop(0, replicas - 1, send, 0)
        for part in range(parts):
            low = range_low(me, part, steps)
            gathered[prefixes - 1, rows_at(low, piece), :] = prefix_ref[rows_at(low, piece), :]

    code_copy.wait()
    issue(4)
    arrived[0] = picked(me)

    m_ref[...] = jnp.full_like(m_ref, -jnp.inf)
    l_ref[...] = jnp.zeros_like(l_ref)
    acc_ref[...] = jnp.zeros_like(acc_ref)

    tokens = q_ref.shape[0]
    for h in range(heads):
        q_rows[h * tokens : (h + 1) * tokens, :] = q_ref[:, h * hd : (h + 1) * hd]

    def attend(key_value, mask_scores=None):
        count = key_value.shape[0]
        scores = lax.dot_general(
            q_rows[...],
            key_value[:, :hd],
            (((1,), (1,)), ((), ())),
            preferred_element_type=jnp.float32,
        )
        if mask_scores is not None:
            scores = mask_scores(scores)
        before = m_ref[...]
        new_max = jnp.maximum(before, jnp.max(scores, axis=1, keepdims=True))
        shrink = jnp.exp2((before - new_max) * coef)
        total = l_ref[...] * shrink
        top = new_max * coef
        weights = []
        for g in range(count // hd):
            w = jnp.exp2(scores[:, g * hd : (g + 1) * hd] * coef - top)
            total = total + w
            weights.append(w.astype(jnp.bfloat16))
        l_ref[...] = total
        m_ref[...] = new_max
        acc_ref[...] = acc_ref[...] * shrink + jnp.dot(
            jnp.concatenate(weights, axis=1),
            key_value[:, hd:],
            preferred_element_type=jnp.float32,
        )

    unit = 256

    def attend_suffix():
        n = suffix_ref.shape[0]
        causal = lax.broadcasted_iota(jnp.int32, (tokens, n), 1) <= lax.broadcasted_iota(
            jnp.int32, (tokens, n), 0
        )

        def masked(scores):
            return jnp.concatenate(
                [
                    jnp.where(causal, scores[h * tokens : (h + 1) * tokens], -jnp.inf)
                    for h in range(heads)
                ],
                axis=0,
            )

        attend(suffix_ref[...], masked)

    def attend_own():
        def piece_of(j, c):
            low = j * unit
            visible = lax.broadcasted_iota(jnp.int32, (1, unit), 1) < ctx_ref[0] - low
            attend(
                own_ref[pl.ds(low, unit), :],
                lambda scores: jnp.where(visible, scores, -jnp.inf),
            )
            return c

        for j in range(own_ref.shape[0] // unit):
            piece_of(j, 0)

    block = arrived.shape[1]
    chunk = unit // block
    groups = list(range(0, replicas, chunk))

    def attend_moved(n):
        n = min(n, len(groups))
        if n == 0:
            return
        first = groups[0]
        del groups[:n]
        for k in range(first, first + n * chunk):
            if k > 0:
                move_copy(k - 1).wait_recv()

        def group(j, c):
            low = first + j * chunk
            flags = jnp.concatenate(
                [
                    arrived[low + k, 0:16, 0:hd].astype(jnp.float32)[0:1]
                    for k in range(chunk)
                    for _ in range(block // hd)
                ],
                axis=1,
            )
            attend(
                arrived[pl.ds(low, chunk)].reshape(unit, 2 * hd),
                lambda scores: jnp.where(flags < LIMIT, scores, -jnp.inf),
            )
            return c

        for j in range(n):
            group(j, 0)

    def attend_prefix(lows):
        for low in lows:
            key_value = gathered[0, rows_at(low, unit), :]
            for p in range(1, prefixes):
                key_value = jnp.where(slot == p, gathered[p, rows_at(low, unit), :], key_value)
            attend(key_value)

    def rs_step(t):
        for part in range(parts):
            rs_copy(t, part).wait()
            rs_take(t, part)
            if t + 1 < steps:
                rs_copy(t + 1, part).start()

    def scatter_wait():
        @pl.when(me != replicas - 1)
        def _():
            for part in range(parts):
                scatter_copy(me, part).wait_recv()

    def ag_begin(fixed):
        for part in range(parts):
            ag_copy(steps - 1, part, fixed).start()

    def ag_step(t, fixed):
        for part in range(parts):
            ag_copy(t, part, fixed).wait()
            if t == 2 and not fixed:
                for half in range(2):
                    half_copy(half, part, 1).start()
            elif t > 1:
                ag_copy(t - 1, part, fixed).start()
            if t == 3 or t == 2:
                eighth_copy(3 - t, part, fixed).start()
            if t == 1:
                core_copy(1, part, fixed).start()

    DYN, FIX = 0, 1
    both = range(parts)
    beside = flip(1)

    def attend_eighths(device, taken):
        if device is not me:
            for part in both:
                for fixed in (DYN, FIX):
                    eighth_copy(taken, part, fixed).wait()
        attend_prefix([eighth(device, part, taken) for part in both])

    step = functools.partial
    merged = [step(rs_step, t) for t in range(steps - 2)]
    merged += [lambda: (scatter_wait(), ag_begin(FIX)), step(rs_step, steps - 2)]
    merged += [step(ag_step, steps - 1, FIX), lambda: (rs_step(steps - 1), ag_begin(DYN))]
    for t in range(steps - 1, 1, -1):
        merged += [step(ag_step, t - 1, FIX), step(ag_step, t, DYN)]
    last = len(merged) - 1
    moved_at = {3: 1, 4: 2, 5: 1, 6: 2, 7: 2, 8: 1, 9: 2, 10: 1, 11: 2}
    for i, event in enumerate(merged):
        event()
        issue(3 if i in (2, 3, 4, 6) else 2)
        if i == 1:
            attend_suffix()
        elif i == 2:
            attend_own()
        attend_moved(moved_at.get(i, 0))
        if i == last - 2:
            attend_eighths(me, 0)
        elif i == last - 1:
            attend_eighths(beside, 0)
    issue(replicas)
    half_rows = part_rows >> 3
    attend_eighths(me, 1)
    attend_eighths(beside, 1)
    attend_moved(len(groups) - 2)
    for part in both:
        core_copy(1, part, FIX).wait()
    for half in range(2):
        for part in both:
            half_copy(half, part, 1).wait()
            half_copy(half, part, 0).start()
        if half == 1:
            attend_moved(2)
        attend_prefix([quarter(me, part, 1) + half * half_rows for part in both])
        for part in both:
            half_copy(half, part, 0).wait()
        attend_prefix([quarter(beside, part, 1) + half * half_rows for part in both])

    for h in range(heads):
        rows = slice(h * tokens, (h + 1) * tokens)
        denominator = jnp.sum(l_ref[rows, :], axis=1, keepdims=True)
        o_ref[:, h * hd : (h + 1) * hd] = (acc_ref[rows, :] / denominator).astype(o_ref.dtype)

    for i in range(replicas - 1):
        move_copy(i).wait_send()

    @pl.when(me == replicas - 1)
    def _():
        def done(target, c):
            for part in range(parts):
                scatter_copy(target, part).wait_send()
            return c

        lax.fori_loop(0, replicas - 1, done, 0)


def on_device(
    queries,
    suffix_kv,
    own_cache,
    ctx_len,
    prefix_cache,
    owners,
    readers,
    kv_pool,
    mig_target,
    mig_block,
    mig_count,
):
    replicas = lax.axis_size("replica")
    hd = suffix_kv.shape[1] // 2
    heads = queries.shape[1] // hd
    tokens = queries.shape[0]
    prefixes = owners.shape[0]
    steps = replicas.bit_length() - 1
    prefix_len, width = prefix_cache.shape
    part_rows = prefix_len // 2
    vmem = pl.BlockSpec(memory_space=pltpu.VMEM)
    smem = pl.BlockSpec(memory_space=pltpu.SMEM)
    dma = pltpu.SemaphoreType.DMA
    return pl.pallas_call(
        functools.partial(attention_kernel, (replicas, prefixes, heads, hd)),
        out_shape=jax.ShapeDtypeStruct(queries.shape, jnp.bfloat16),
        in_specs=[smem] * 4 + [vmem] * 5 + [pl.BlockSpec(memory_space=pl.ANY)] * 2,
        out_specs=vmem,
        scratch_shapes=[
            pltpu.VMEM(prefix_cache.shape, jnp.bfloat16),
            pltpu.VMEM(kv_pool.shape, jnp.bfloat16),
            pltpu.VMEM((prefixes, prefix_len, width), jnp.bfloat16),
            pltpu.VMEM((prefixes - 1, prefix_len, width), jnp.bfloat16),
            pltpu.VMEM((2, part_rows // 2, width), jnp.bfloat16),
            pltpu.VMEM((2, prefixes - 1, part_rows // 2, width), jnp.bfloat16),
            pltpu.VMEM((replicas,) + kv_pool.shape[1:], jnp.bfloat16),
            pltpu.VMEM((replicas,) + kv_pool.shape[1:], jnp.bfloat16),
            pltpu.VMEM((replicas, 128), jnp.int32),
            pltpu.SMEM((replicas, 128), jnp.int32),
            pltpu.VMEM((heads * tokens, hd), jnp.bfloat16),
            pltpu.VMEM((heads * tokens, hd), jnp.float32),
            pltpu.VMEM((heads * tokens, hd), jnp.float32),
            pltpu.VMEM((heads * tokens, hd), jnp.float32),
            dma((steps, 2)),
            dma((steps, 2)),
            dma((steps, 2, 2)),
            dma((steps, 2, 2)),
            dma((replicas, 2)),
            dma((2,)),
            dma((replicas,)),
            dma((replicas,)),
            dma((2, 2, 2)),
            dma((2, 2, 2)),
            dma,
            dma((2,)),
            dma((2, 2, 2)),
            dma((2, 2, 2)),
            dma((2, 2, 2)),
            dma((2, 2, 2)),
        ],
        compiler_params=pltpu.CompilerParams(
            collective_id=0, has_side_effects=True, vmem_limit_bytes=56 * 1024 * 1024
        ),
    )(
        ctx_len,
        owners,
        readers,
        mig_count,
        mig_target,
        mig_block,
        queries,
        suffix_kv,
        own_cache,
        prefix_cache,
        kv_pool,
    )


def solution(mesh):
    in_specs = (
        P(("groups", "replica"), None),
        P(("groups", "replica"), None),
        P(("groups", "replica"), None),
        P(("groups", "replica")),
        P(("groups", "replica"), None),
        P("groups"),
        P("groups"),
        P(("groups", "replica"), None, None),
        P(("groups", "replica"), None),
        P(("groups", "replica"), None),
        P(("groups", "replica")),
    )
    out_specs = P(("groups", "replica"), None)
    return jax.shard_map(
        on_device, mesh=mesh, in_specs=in_specs, out_specs=out_specs, check_vma=False
    )
```
